32 devices in a mesh: gy: 4 (over x, core), gx: 4 (over z), probe: 2 (over y).
Axes of the slice: x: 2, y: 2, z: 4, core: 2. Of those that a mesh axis runs over, the one named last changes fastest.
Arguments:
- state: bfloat16 [4, 16, 16, 640], P(None, 'gy', 'gx'), may hold values from -6 to 6
- probe_signs: int32 [4, 4, 16, 16, 640], P('probe', None, 'gy', 'gx'), may hold values from -1 to 1, as said below
- timesteps: int32 [4], replicated, may hold values from 0 to 999
- time_table: float32 [1000, 640], replicated, may hold values from -4 to 4
- gn_gain: float32 [640], replicated, may hold values from 0.5 to 1.5
- gn_shift: float32 [640], replicated, may hold values from -3 to 3
- conv_weight: bfloat16 [9, 640, 640], P(None, 'probe'), may hold values from -0.078125 to 0.078125
- conv_bias: float32 [640], replicated, may hold values from -3 to 3
Outputs:
- next_state: bfloat16 [4, 16, 16, 640], P(None, 'gy', 'gx')
- logp_delta: float32 [4], replicated
The draws below stay inside these ranges and needn't reach their ends.
Inputs may be any that keep to these rules, and one draw needn't show every extreme that they name: `probe_signs`: every entry is -1 or 1.
All inputs are finite; a program needn't handle non-finite values.
Results may differ from the reference program's by a relative error of at most 0.0034.
Values may be sent and summed in bfloat16 or wider, within the bound.
A program may use at most 64 MiB of HBM per device.

```python
import jax
import jax.numpy as jnp
from jax import lax

C = 640
GROUPS = 32
STEPS = 1000
BATCH = 4
PROBES = 4
H = 16
W = 16


def draw_probe_signs(key, part):
    bits = jax.random.randint(key, (PROBES, BATCH, H, W, C), 0, 2, dtype=jnp.int32)
    return bits * 2 - 1


def plant(result, key, least, largest):
    longest = result.shape.index(max(result.shape))
    spots = []
    for shift in (0, 1):
        where = [jax.random.randint(jax.random.fold_in(key, axis), (), 0, length) for axis, length in enumerate(result.shape)]
        where[longest] = (where[longest] + shift) % result.shape[longest]
        spots.append(tuple(where))
    return result.at[spots[0]].set(least).at[spots[1]].set(largest)


def shard_levels(stream_key, extent, shards, least, top_value):
    def one(position, parts):
        heights = jax.random.uniform(jax.random.fold_in(jax.random.fold_in(stream_key, 6), position), (parts,), jnp.float32, least / len(shards), top_value / len(shards))
        return jnp.repeat(jnp.exp(heights), extent[position] // parts).reshape((-1,) + (1,) * (len(extent) - position - 1))

    gain = one(*shards[0])
    for cut in shards[1:]:
        gain = gain * one(*cut)
    return gain


def normal_values(key, extent, scale, most, pieces=(), kind=jnp.bfloat16):
    loudness = shard_levels(key, extent, pieces, -0.22, 0.18) if pieces else 1.0
    result = jax.random.normal(key, extent, jnp.float32) * scale * loudness
    return jnp.minimum(jnp.maximum(result, -most), most).astype(kind)


def setup_inputs(seed: int = 0) -> dict:
    key_of = jax.random.split(jax.random.key(seed), 9)
    state = normal_values(key_of[0], (BATCH, H, W, C), 1.0, 6.0, ((1, 4), (2, 4)))
    probe_signs = draw_probe_signs(jax.random.fold_in(key_of[8], 71), 0)
    timesteps = plant(jax.random.randint(key_of[2], (BATCH,), 0, STEPS), jax.random.fold_in(key_of[2], 1), 0, STEPS - 1).astype(jnp.int32)
    time_table = normal_values(key_of[3], (STEPS, C), 0.5, 4.0, (), jnp.float32)
    gn_gain = jnp.clip(1.0 + 0.1 * jax.random.normal(key_of[4], (C,), jnp.float32), 0.5, 1.5)
    gn_shift = normal_values(key_of[5], (C,), 0.5, 3.0, (), jnp.float32)
    conv_weight = normal_values(key_of[6], (9, C, C), (9 * C) ** -0.5, 0.078125, ((1, 2),))
    conv_bias = normal_values(key_of[7], (C,), 0.5, 3.0, (), jnp.float32)
    return {"state": state, "probe_signs": probe_signs, "timesteps": timesteps, "time_table": time_table, "gn_gain": gn_gain, "gn_shift": gn_shift, "conv_weight": conv_weight, "conv_bias": conv_bias}


def convolve(stack, weight):
    padded = jnp.pad(stack, ((0, 0), (1, 1), (1, 1), (0, 0)))
    count, height, width, chans = stack.shape
    total = jnp.zeros((count * height * width, weight.shape[2]), jnp.float32)
    for tap in range(9):
        row_off = tap // 3
        col_off = tap % 3
        window = padded[:, row_off:row_off + height, col_off:col_off + width, :].reshape(-1, chans)
        total = total + jnp.dot(window, weight[tap], preferred_element_type=jnp.float32)
    return total.reshape(count, height, width, weight.shape[2])

def reference(state, probe_signs, timesteps, time_table, gn_gain, gn_shift, conv_weight, conv_bias):
    batch, height, width, chans = state.shape
    group_width = chans // GROUPS
    count = height * width * group_width
    xf = state.astype(jnp.float32)
    grouped = xf.reshape(batch, height, width, GROUPS, group_width)
    mean_x = lax.optimization_barrier(jnp.sum(grouped, axis=(1, 2, 4))) / count
    var_x = lax.optimization_barrier(jnp.sum(grouped * grouped, axis=(1, 2, 4))) / count - mean_x * mean_x
    sigma = jnp.sqrt(var_x + 1e-05)[:, None, None, :, None]
    centered = grouped - mean_x[:, None, None, :, None]
    normal = (centered / sigma).reshape(batch, height, width, chans)
    embed = time_table[timesteps]
    pre = normal * gn_gain + gn_shift + embed[:, None, None, :]
    sig = jax.nn.sigmoid(pre)
    hidden = (pre * sig).astype(jnp.bfloat16)
    slope = sig * (1.0 + pre * (1.0 - sig)) * gn_gain
    velocity = convolve(hidden, conv_weight) + conv_bias
    next_state = (xf + 0.25 * velocity).astype(jnp.bfloat16)

    def one_probe(signs):
        ug = signs.astype(jnp.float32).reshape(batch, height, width, GROUPS, group_width)
        mean_u = lax.optimization_barrier(jnp.sum(ug, axis=(1, 2, 4))) / count
        mean_cu = lax.optimization_barrier(jnp.sum(ug * centered, axis=(1, 2, 4))) / count
        dnormal = (ug - mean_u[:, None, None, :, None]) / sigma - centered * mean_cu[:, None, None, :, None] / (sigma * sigma * sigma)
        dhidden = (slope * dnormal.reshape(batch, height, width, chans)).astype(jnp.bfloat16)
        tangent = convolve(dhidden, conv_weight)
        return lax.optimization_barrier(jnp.sum(signs.astype(jnp.float32) * tangent, axis=(1, 2, 3)))
    partials = lax.map(one_probe, probe_signs)
    logp_delta = -0.25 / probe_signs.shape[0] * lax.optimization_barrier(jnp.sum(partials, axis=0))
    return (next_state, logp_delta)
```

```python
import jax
import jax.numpy as jnp
from jax import lax
from jax.sharding import PartitionSpec as P

GROUPS = 32


def with_halo(block, sides, width):
    for axis, dim in sides:
        count = lax.axis_size(axis)
        forward = [(i, i + 1) for i in range(count - 1)]
        backward = [(target, source) for source, target in forward]
        low = lax.ppermute(
            lax.slice_in_dim(block, block.shape[dim] - width, None, axis=dim), axis, forward
        )
        high = lax.ppermute(lax.slice_in_dim(block, 0, width, axis=dim), axis, backward)
        block = jnp.concatenate([low, block, high], axis=dim)
    return block


def local_conv(padded, weight, height, width):
    count = padded.shape[0]
    chans = padded.shape[3]
    total = jnp.zeros((count * height * width, weight.shape[2]), jnp.float32)
    for tap in range(9):
        row_off = tap // 3
        col_off = tap % 3
        window = padded[:, row_off : row_off + height, col_off : col_off + width, :].reshape(
            -1, chans
        )
        total = total + jnp.dot(window, weight[tap], preferred_element_type=jnp.float32)
    return total


def travelling_probes(state, probe_signs, timesteps, time_table, gn_gain, gn_shift, conv_weight, conv_bias):
    batch, tile_h, tile_w, chans = state.shape
    share = conv_weight.shape[1]
    group_width = chans // GROUPS
    ny, nx = lax.axis_size("gy"), lax.axis_size("gx")
    count = tile_h * ny * tile_w * nx * group_width
    xf = state.astype(jnp.float32)
    signs = lax.all_gather(probe_signs.astype(jnp.bfloat16), "probe", axis=0, tiled=True)
    probes = signs.shape[0]
    first = lax.axis_index("probe") * share

    def mine(array):
        return lax.dynamic_slice_in_dim(array, first, share, axis=array.ndim - 1)

    stacked = jnp.concatenate([state[None], signs], axis=0)
    stacked = mine(stacked).reshape((1 + probes) * batch, tile_h, tile_w, share)
    padded = with_halo(stacked, (("gy", 1), ("gx", 2)), 1)
    padded = padded.reshape(1 + probes, batch, tile_h + 2, tile_w + 2, share).astype(jnp.float32)

    cells_x = jnp.stack([jnp.sum(xf, axis=(1, 2)), jnp.sum(xf * xf, axis=(1, 2))])
    signs_f = signs.astype(jnp.float32)
    cells_u = jnp.stack([jnp.sum(signs_f, axis=(2, 3)), jnp.sum(signs_f * xf[None], axis=(2, 3))])
    cells = jnp.concatenate([cells_x, cells_u.reshape(2 * probes, batch, chans)], axis=0)
    sums = jnp.sum(cells.reshape(2 + 2 * probes, batch, GROUPS, group_width), axis=3)
    sums = lax.psum(sums, ("gy", "gx")) / count
    mean_x, mean_xx = sums[0], sums[1]
    mean_u, cross = sums[2 : 2 + probes], sums[2 + probes :]
    sigma = jnp.sqrt(mean_xx - mean_x * mean_x + 1e-05)
    mean_cu = cross - mean_x[None] * mean_u
    inv = 1.0 / sigma
    table = jnp.concatenate([mean_x[None], inv[None], mean_u, mean_cu * (inv * inv * inv)], axis=0)
    table = mine(jnp.repeat(table, group_width, axis=2))[:, :, None, None, :]

    onehot = (
        timesteps[:, None] == jnp.arange(time_table.shape[0], dtype=jnp.int32)[None, :]
    ).astype(jnp.float32)
    embed = jnp.dot(onehot, time_table, precision=lax.Precision.HIGHEST)
    offset = mine(gn_shift + embed)[:, None, None, :]
    gain = mine(gn_gain)
    centered = padded[0] - table[0]
    pre = centered * table[1] * gain + offset
    sig = jax.nn.sigmoid(pre)
    rows = lax.axis_index("gy") * tile_h - 1 + jnp.arange(tile_h + 2)
    cols = lax.axis_index("gx") * tile_w - 1 + jnp.arange(tile_w + 2)
    inside = ((rows >= 0) & (rows < tile_h * ny))[:, None] & (
        (cols >= 0) & (cols < tile_w * nx)
    )[None, :]
    inside = inside[:, :, None]
    hidden = jnp.where(inside, pre * sig, 0.0).astype(jnp.bfloat16)
    slope = jnp.where(inside, sig * (1.0 + pre * (1.0 - sig)) * gain, 0.0)
    dnormal = (padded[1:] - table[2 : 2 + probes]) * table[1] - centered * table[2 + probes :]
    dhidden = (slope[None] * dnormal).astype(jnp.bfloat16)

    velocity = local_conv(hidden, conv_weight, tile_h, tile_w)
    velocity = lax.psum(velocity, "probe").reshape(batch, tile_h, tile_w, chans) + conv_bias
    next_state = (xf + 0.25 * velocity).astype(jnp.bfloat16)
    tangent = local_conv(
        dhidden.reshape(probes * batch, tile_h + 2, tile_w + 2, share), conv_weight, tile_h, tile_w
    ).reshape(signs.shape)
    total = lax.psum(jnp.sum(signs_f * tangent, axis=(0, 2, 3, 4)), ("gy", "gx", "probe"))
    return (next_state, -0.25 / probes * total)


def gathered_weights(state, probe_signs, timesteps, time_table, gn_gain, gn_shift, conv_weight, conv_bias):
    batch, tile_h, tile_w, chans = state.shape
    probes_here = probe_signs.shape[0]
    group_width = chans // GROUPS
    count = tile_h * lax.axis_size("gy") * tile_w * lax.axis_size("gx") * group_width
    xf = state.astype(jnp.float32)
    signs = probe_signs.astype(jnp.float32)
    grouped = xf.reshape(batch, tile_h, tile_w, GROUPS, group_width)
    signs_grouped = signs.reshape(probes_here, batch, tile_h, tile_w, GROUPS, group_width)
    sum_x = jnp.sum(grouped, axis=(1, 2, 4))
    sum_xx = jnp.sum(grouped * grouped, axis=(1, 2, 4))
    sum_u = jnp.sum(signs_grouped, axis=(2, 3, 5))
    cross = jnp.sum(signs_grouped * grouped[None], axis=(2, 3, 5))
    sum_x, sum_xx, sum_u, cross = lax.psum((sum_x, sum_xx, sum_u, cross), ("gy", "gx"))
    mean_x = sum_x / count
    centered = grouped - mean_x[:, None, None, :, None]
    sum_cu = cross - mean_x[None] * sum_u
    var_x = sum_xx / count - mean_x * mean_x
    sigma = jnp.sqrt(var_x + 1e-05)[:, None, None, :, None]
    normal = (centered / sigma).reshape(batch, tile_h, tile_w, chans)
    mean_u = (sum_u / count)[:, :, None, None, :, None]
    mean_cu = (sum_cu / count)[:, :, None, None, :, None]
    dnormal = (signs_grouped - mean_u) / sigma[None] - centered[None] * mean_cu / (
        sigma * sigma * sigma
    )[None]
    dnormal = dnormal.reshape(probes_here, batch, tile_h, tile_w, chans)
    onehot = (
        timesteps[:, None] == jnp.arange(time_table.shape[0], dtype=jnp.int32)[None, :]
    ).astype(jnp.float32)
    embed = jnp.dot(onehot, time_table, precision=lax.Precision.HIGHEST)
    pre = normal * gn_gain + gn_shift + embed[:, None, None, :]
    sig = jax.nn.sigmoid(pre)
    hidden = (pre * sig).astype(jnp.bfloat16)
    slope = sig * (1.0 + pre * (1.0 - sig)) * gn_gain
    dhidden = (slope[None] * dnormal).astype(jnp.bfloat16)
    flat_tangents = dhidden.reshape(probes_here * batch, tile_h, tile_w, chans)
    stacked = jnp.concatenate([hidden, flat_tangents], axis=0)
    items = stacked.shape[0]
    padded = with_halo(stacked, (("gy", 1), ("gx", 2)), 1)
    summed = local_conv(
        padded, lax.all_gather(conv_weight, "probe", axis=1, tiled=True), tile_h, tile_w
    )
    conv_out = summed.reshape(items, tile_h, tile_w, chans)
    conv_primal = conv_out[:batch]
    tangent = conv_out[batch:].reshape(probes_here, batch, tile_h, tile_w, chans)
    partial_sum = jnp.sum(signs * tangent, axis=(0, 2, 3, 4))
    velocity = conv_primal + conv_bias
    next_state = (xf + 0.25 * velocity).astype(jnp.bfloat16)
    total = lax.psum(partial_sum, ("gy", "gx", "probe"))
    logp_delta = -0.25 / (probes_here * lax.axis_size("probe")) * total
    return (next_state, logp_delta)


def solution(mesh):
    def body(*args):
        wide = args[6].shape[1] >= 128
        return (travelling_probes if wide else gathered_weights)(*args)

    in_specs = (
        P(None, "gy", "gx", None),
        P("probe", None, "gy", "gx", None),
        P(),
        P(),
        P(),
        P(),
        P(None, "probe", None),
        P(),
    )
    out_specs = (P(None, "gy", "gx", None), P())
    return jax.shard_map(body, mesh=mesh, in_specs=in_specs, out_specs=out_specs, check_vma=False)
```

```python
import functools

import jax
import jax.numpy as jnp
from jax import lax
from jax.experimental import pallas as pl
from jax.experimental.pallas import tpu as pltpu
from jax.sharding import PartitionSpec as P

GROUPS = 32


def with_halo(block, sides, width):
    for axis, dim in sides:
        count = lax.axis_size(axis)
        forward = [(i, i + 1) for i in range(count - 1)]
        backward = [(target, source) for source, target in forward]
        low = lax.ppermute(
            lax.slice_in_dim(block, block.shape[dim] - width, None, axis=dim), axis, forward
        )
        high = lax.ppermute(lax.slice_in_dim(block, 0, width, axis=dim), axis, backward)
        block = jnp.concatenate([low, block, high], axis=dim)
    return block


def local_conv(padded, weight, height, width):
    count = padded.shape[0]
    chans = padded.shape[3]
    total = jnp.zeros((count * height * width, weight.shape[2]), jnp.float32)
    for tap in range(9):
        row_off = tap // 3
        col_off = tap % 3
        window = padded[:, row_off : row_off + height, col_off : col_off + width, :].reshape(
            -1, chans
        )
        total = total + jnp.dot(window, weight[tap], preferred_element_type=jnp.float32)
    return total


def gathered_weights(state, probe_signs, timesteps, time_table, gn_gain, gn_shift, conv_weight, conv_bias):
    batch, tile_h, tile_w, chans = state.shape
    probes_here = probe_signs.shape[0]
    group_width = chans // GROUPS
    count = tile_h * lax.axis_size("gy") * tile_w * lax.axis_size("gx") * group_width
    xf = state.astype(jnp.float32)
    signs = probe_signs.astype(jnp.float32)
    grouped = xf.reshape(batch, tile_h, tile_w, GROUPS, group_width)
    signs_grouped = signs.reshape(probes_here, batch, tile_h, tile_w, GROUPS, group_width)
    sum_x = jnp.sum(grouped, axis=(1, 2, 4))
    sum_xx = jnp.sum(grouped * grouped, axis=(1, 2, 4))
    sum_u = jnp.sum(signs_grouped, axis=(2, 3, 5))
    cross = jnp.sum(signs_grouped * grouped[None], axis=(2, 3, 5))
    sum_x, sum_xx, sum_u, cross = lax.psum((sum_x, sum_xx, sum_u, cross), ("gy", "gx"))
    mean_x = sum_x / count
    centered = grouped - mean_x[:, None, None, :, None]
    sum_cu = cross - mean_x[None] * sum_u
    var_x = sum_xx / count - mean_x * mean_x
    sigma = jnp.sqrt(var_x + 1e-05)[:, None, None, :, None]
    normal = (centered / sigma).reshape(batch, tile_h, tile_w, chans)
    mean_u = (sum_u / count)[:, :, None, None, :, None]
    mean_cu = (sum_cu / count)[:, :, None, None, :, None]
    dnormal = (signs_grouped - mean_u) / sigma[None] - centered[None] * mean_cu / (
        sigma * sigma * sigma
    )[None]
    dnormal = dnormal.reshape(probes_here, batch, tile_h, tile_w, chans)
    onehot = (
        timesteps[:, None] == jnp.arange(time_table.shape[0], dtype=jnp.int32)[None, :]
    ).astype(jnp.float32)
    embed = jnp.dot(onehot, time_table, precision=lax.Precision.HIGHEST)
    pre = normal * gn_gain + gn_shift + embed[:, None, None, :]
    sig = jax.nn.sigmoid(pre)
    hidden = (pre * sig).astype(jnp.bfloat16)
    slope = sig * (1.0 + pre * (1.0 - sig)) * gn_gain
    dhidden = (slope[None] * dnormal).astype(jnp.bfloat16)
    flat_tangents = dhidden.reshape(probes_here * batch, tile_h, tile_w, chans)
    stacked = jnp.concatenate([hidden, flat_tangents], axis=0)
    items = stacked.shape[0]
    padded = with_halo(stacked, (("gy", 1), ("gx", 2)), 1)
    summed = local_conv(
        padded, lax.all_gather(conv_weight, "probe", axis=1, tiled=True), tile_h, tile_w
    )
    conv_out = summed.reshape(items, tile_h, tile_w, chans)
    conv_primal = conv_out[:batch]
    tangent = conv_out[batch:].reshape(probes_here, batch, tile_h, tile_w, chans)
    partial_sum = jnp.sum(signs * tangent, axis=(0, 2, 3, 4))
    velocity = conv_primal + conv_bias
    next_state = (xf + 0.25 * velocity).astype(jnp.bfloat16)
    total = lax.psum(partial_sum, ("gy", "gx", "probe"))
    logp_delta = -0.25 / (probes_here * lax.axis_size("probe")) * total
    return (next_state, logp_delta)


MESH = pl.DeviceIdType.MESH
F32 = jnp.float32
BF16 = jnp.bfloat16


def exact_dot(a, b):
    return jnp.dot(a, b, precision=lax.Precision.HIGHEST, preferred_element_type=F32)


def kernel(
    ny, nx, u_ref, x_ref, coef_ref, w_hbm, v_out, l_out,
    w_ref, halo, same, other, peer, acts, line, plane, vel, vel_in, line2, plane2,
    w_sem, send, recv,
):
    gy, gx, me = lax.axis_index("gy"), lax.axis_index("gx"), lax.axis_index("probe")
    tile_h, tile_w, rows, chans = u_ref.shape
    share = w_ref.shape[1]
    batch = vel.shape[1]
    cells = tile_h * tile_w
    width = chans // GROUPS
    count = cells * ny * nx * width
    w_copy = pltpu.make_async_copy(w_hbm, w_ref, w_sem)
    w_copy.start()

    def half(array, which):
        return jnp.where(which == 0, array, pltpu.roll(array, share, 1))[:, :share]

    def spots(step, size, landing):
        if step == 0:
            return pl.ds(1, size) if landing else pl.ds(0, size)
        if landing:
            return pl.ds(0, 1) if step > 0 else pl.ds(size + 1, 1)
        return pl.ds(size - 1, 1) if step > 0 else pl.ds(0, 1)

    def exists(dy, dx):
        y, x = gy + dy, gx + dx
        return (y >= 0) & (y < ny) & (x >= 0) & (x < nx)

    compass = [(dy, dx) for dy in (-1, 0, 1) for dx in (-1, 0, 1) if dy or dx]

    for slot in range(3):
        halo[slot] = jnp.zeros(halo.shape[1:], BF16)
    barrier = pltpu.get_barrier_semaphore()
    line_mates = [(gy, lax.rem(gx + k, nx), me) for k in range(1, nx)]
    plane_mates = [
        (lax.rem(gy + k, ny), gx, lax.rem(me + q, 2))
        for k in range(ny) for q in range(2) if k or q
    ]
    extra = [(dy, dx, q) for dy, dx in compass for q in range(2) if dx and (dy or q)]
    for mate in line_mates + plane_mates:
        pl.semaphore_signal(barrier, inc=1, device_id=mate, device_id_type=MESH)
    for dy, dx, q in extra:
        @pl.when(exists(dy, dx))
        def _():
            pl.semaphore_signal(
                barrier, inc=1, device_id=(gy + dy, gx + dx, lax.rem(me + q, 2)),
                device_id_type=MESH,
            )

    u = u_ref[...].astype(F32).reshape(cells, rows, chans)
    x = x_ref[...].astype(F32).reshape(cells, rows, chans)
    box = (tile_h, tile_w, rows, share)
    inner = (pl.ds(1, tile_h), pl.ds(1, tile_w))
    x_mine = half(x.reshape(cells * rows, chans), me).reshape(box).astype(BF16)
    u_flat = u.reshape(cells * rows, chans)
    u_mine = half(u_flat, me).reshape(box).astype(BF16)
    same[0] = x_mine
    same[1] = u_mine
    halo[(0,) + inner] = x_mine
    halo[(1,) + inner] = u_mine
    other[...] = half(u_flat, 1 - me).reshape(box).astype(BF16)
    sums = jnp.concatenate(
        [jnp.sum(x, 0), jnp.sum(x * x, 0), jnp.sum(u, 0), jnp.sum(u * x, 0)], axis=0
    )
    lanes = 128
    chan = lax.broadcasted_iota(jnp.int32, (chans, lanes), 0)
    group = lax.broadcasted_iota(jnp.int32, (chans, lanes), 1) * width
    pick = ((chan >= group) & (chan < group + width)).astype(F32)
    per_group = exact_dot(sums, pick)
    local = per_group[:rows]
    for k in range(1, 4):
        local = local + pltpu.roll(per_group[k * rows : (k + 1) * rows], GROUPS * k, 1)
    line[gx] = local

    greeted = len(line_mates) + len(plane_mates)
    for dy, dx, q in extra:
        greeted = greeted + jnp.where(exists(dy, dx), 1, 0)
    pl.semaphore_wait(barrier, greeted)

    taken = [0]

    def remote(src, dst, device):
        taken[0] += 1
        at = taken[0] - 1
        return pltpu.make_async_remote_copy(
            src_ref=src, dst_ref=dst, send_sem=send.at[at], recv_sem=recv.at[at],
            device_id=device, device_id_type=MESH,
        )

    def to_all(src, dst, mates):
        copies = [remote(src, dst, mate) for mate in mates]
        for copy in copies:
            copy.start()
        return copies

    line_copies = to_all(line.at[gx], line.at[gx], line_mates)
    tile_copy = remote(u_ref, peer, (gy, gx, 1 - me))
    tile_copy.start()
    rims = []
    for dy, dx in compass:
        src = (spots(dy, tile_h, False), spots(dx, tile_w, False))
        dst = (spots(dy, tile_h, True), spots(dx, tile_w, True))
        both = [
            remote(
                same.at[(slice(None),) + src], halo.at[(pl.ds(0, 2),) + dst],
                (gy + dy, gx + dx, me),
            ),
            remote(other.at[src], halo.at[(2,) + dst], (gy + dy, gx + dx, 1 - me)),
        ]
        rims.append((dy, dx, both))

        @pl.when(exists(dy, dx))
        def _():
            for copy in both:
                copy.start()

    for copy in line_copies:
        copy.wait()
    total = line[0]
    for k in range(1, nx):
        total = total + line[k]
    plane[gy, me] = total
    plane_copies = to_all(plane.at[gy, me], plane.at[gy, me], plane_mates)
    for copy in plane_copies:
        copy.wait()

    def moments(which):
        total = plane[0, which]
        for k in range(1, ny):
            total = total + plane[k, which]
        total = total / count
        valid = lax.broadcasted_iota(jnp.int32, total.shape, 1) < GROUPS
        return [
            jnp.where(valid, total if k == 0 else pltpu.roll(total, lanes - GROUPS * k, 1), 0.0)
            for k in range(4)
        ]

    mean_x, mean_xx, mean_u, cross = moments(me)
    _, _, mean_v, cross_v = moments(1 - me)
    inv = 1.0 / jnp.sqrt(mean_xx - mean_x * mean_x + 1e-05)
    cube = inv * inv * inv
    table = jnp.concatenate(
        [mean_x, inv, mean_u, (cross - mean_x * mean_u) * cube, mean_v,
         (cross_v - mean_x * mean_v) * cube], axis=0,
    )
    chan = lax.broadcasted_iota(jnp.int32, (lanes, share), 1) + me * share
    group = lax.broadcasted_iota(jnp.int32, (lanes, share), 0) * width
    spread = ((chan >= group) & (chan < group + width)).astype(F32)
    table = exact_dot(table, spread)
    mean_x, inv, mean_u, mean_cu, mean_v, mean_cv = [
        table[k * rows : (k + 1) * rows] for k in range(6)
    ]
    coef = half(coef_ref[...], me)
    offset, gain = coef[:rows], coef[rows:]

    tile_copy.wait()
    halo[(2,) + inner] = (
        half(peer[...].astype(F32).reshape(cells * rows, chans), me).reshape(box).astype(BF16)
    )
    for dy, dx, both in rims:
        @pl.when(exists(dy, dx))
        def _():
            for copy in both:
                copy.wait_send()

        @pl.when(exists(-dy, -dx))
        def _():
            for copy in both:
                copy.wait_recv()

    for y in range(tile_h + 2):
        centered = halo[0, y].astype(F32) - mean_x
        normal = centered * inv
        pre = normal * gain + offset
        sig = 1.0 / (1.0 + jnp.exp(-pre))
        slope = sig * (1.0 + pre * (1.0 - sig)) * gain
        acts[y, :, 0:rows] = pre * sig
        acts[y, :, rows : 2 * rows] = slope * (
            (halo[1, y].astype(F32) - mean_u) * inv - centered * mean_cu
        )
        acts[y, :, 2 * rows :] = slope * (
            (halo[2, y].astype(F32) - mean_v) * inv - centered * mean_cv
        )
    for edge, at in (
        (gy == 0, (0,)), (gy == ny - 1, (tile_h + 1,)),
        (gx == 0, (slice(None), 0)), (gx == nx - 1, (slice(None), tile_w + 1)),
    ):
        @pl.when(edge)
        def _():
            acts[at] = jnp.zeros(acts.at[at].shape, F32)

    def conv(first, size):
        total = None
        for tap in range(9):
            dy, dx = tap // 3, tap % 3
            window = acts[dy : dy + tile_h, dx : dx + tile_w, first : first + size]
            window = window.reshape(cells * size, share).astype(BF16)
            part = jnp.dot(window, w_ref[tap], preferred_element_type=F32)
            total = part if total is None else total + part
        return total.reshape(cells, size, chans)

    w_copy.wait()
    vel[...] = conv(0, rows)[:, :batch]
    vel_copy = remote(vel, vel_in, (gy, gx, 1 - me))
    vel_copy.start()
    tangent = conv(rows, 2 * rows)
    u = u_ref[...].astype(F32).reshape(cells, rows, chans)
    v = peer[...].astype(F32).reshape(cells, rows, chans)
    product = jnp.sum(u * tangent[:, :rows] + v * tangent[:, rows:], axis=0)
    folded = product[:, :lanes]
    for k in range(1, chans // lanes):
        folded = folded + product[:, k * lanes : (k + 1) * lanes]
    line2[gx] = folded
    copies = to_all(line2.at[gx], line2.at[gx], line_mates)
    for copy in copies:
        copy.wait()
    total = line2[0]
    for k in range(1, nx):
        total = total + line2[k]
    plane2[gy, me] = total
    copies = to_all(plane2.at[gy, me], plane2.at[gy, me], plane_mates)
    vel_copy.wait()
    v_out[...] = vel[...] + vel_in[...]
    for copy in copies:
        copy.wait()
    total = None
    for y in range(ny):
        for q in range(2):
            total = plane2[y, q] if total is None else total + plane2[y, q]
    l_out[...] = total


def one_kernel(state, probe_signs, timesteps, time_table, gn_gain, gn_shift, conv_weight, conv_bias):
    batch, tile_h, tile_w, chans = state.shape
    probes = probe_signs.shape[0]
    share = conv_weight.shape[1]
    ny, nx = lax.axis_size("gy"), lax.axis_size("gx")
    rows = probes * batch
    u = probe_signs.transpose(2, 3, 0, 1, 4).reshape(tile_h, tile_w, rows, chans).astype(BF16)
    x = jnp.tile(state.transpose(1, 2, 0, 3), (1, 1, probes, 1))
    embed = jnp.concatenate(
        [lax.dynamic_slice_in_dim(time_table, timesteps[b], 1, 0) for b in range(batch)], axis=0
    )
    coef = jnp.concatenate(
        [jnp.tile(embed + gn_shift, (probes, 1)), jnp.broadcast_to(gn_gain, (rows, chans))], axis=0
    )
    copies = 2 * (nx - 1) + 2 * (2 * ny - 1) + 2 + 16
    vmem = pl.BlockSpec(memory_space=pltpu.VMEM)
    velocity, partial = pl.pallas_call(
        functools.partial(kernel, ny, nx),
        out_shape=(
            jax.ShapeDtypeStruct((tile_h * tile_w, batch, chans), F32),
            jax.ShapeDtypeStruct((rows, 128), F32),
        ),
        in_specs=[vmem, vmem, vmem, pl.BlockSpec(memory_space=pl.ANY)],
        out_specs=(vmem, vmem),
        scratch_shapes=[
            pltpu.VMEM(conv_weight.shape, BF16),
            pltpu.VMEM((3, tile_h + 2, tile_w + 2, rows, share), BF16),
            pltpu.VMEM((2, tile_h, tile_w, rows, share), BF16),
            pltpu.VMEM((tile_h, tile_w, rows, share), BF16),
            pltpu.VMEM((tile_h, tile_w, rows, chans), BF16),
            pltpu.VMEM((tile_h + 2, tile_w + 2, 3 * rows, share), F32),
            pltpu.VMEM((nx, rows, 128), F32),
            pltpu.VMEM((ny, 2, rows, 128), F32),
            pltpu.VMEM((tile_h * tile_w, batch, chans), F32),
            pltpu.VMEM((tile_h * tile_w, batch, chans), F32),
            pltpu.VMEM((nx, rows, 128), F32),
            pltpu.VMEM((ny, 2, rows, 128), F32),
            pltpu.SemaphoreType.DMA,
            pltpu.SemaphoreType.DMA((copies,)),
            pltpu.SemaphoreType.DMA((copies,)),
        ],
        compiler_params=pltpu.CompilerParams(collective_id=0, has_side_effects=True),
    )(u, x, coef, conv_weight)
    velocity = velocity.reshape(tile_h, tile_w, batch, chans).transpose(2, 0, 1, 3) + conv_bias
    next_state = (state.astype(F32) + 0.25 * velocity).astype(BF16)
    total = jnp.sum(partial.reshape(probes, batch, 128), axis=(0, 2))
    return (next_state, -0.25 / (2 * probes) * total)


def solution(mesh):
    def body(*args):
        wide = mesh.shape["probe"] == 2 and args[6].shape[1] >= 128
        rows = args[1].shape[0] * args[0].shape[0]
        return (one_kernel if wide and rows == 8 else gathered_weights)(*args)

    in_specs = (
        P(None, "gy", "gx", None),
        P("probe", None, "gy", "gx", None),
        P(),
        P(),
        P(),
        P(),
        P(None, "probe", None),
        P(),
    )
    out_specs = (P(None, "gy", "gx", None), P())
    return jax.shard_map(body, mesh=mesh, in_specs=in_specs, out_specs=out_specs, check_vma=False)
```

```python
import functools

import jax
import jax.numpy as jnp
from jax import lax
from jax.experimental import pallas as pl
from jax.experimental.pallas import tpu as pltpu
from jax.sharding import PartitionSpec as P

GROUPS = 32


def with_halo(block, sides, width):
    for axis, dim in sides:
        count = lax.axis_size(axis)
        forward = [(i, i + 1) for i in range(count - 1)]
        backward = [(target, source) for source, target in forward]
        low = lax.ppermute(
            lax.slice_in_dim(block, block.shape[dim] - width, None, axis=dim), axis, forward
        )
        high = lax.ppermute(lax.slice_in_dim(block, 0, width, axis=dim), axis, backward)
        block = jnp.concatenate([low, block, high], axis=dim)
    return block


def local_conv(padded, weight, height, width):
    count = padded.shape[0]
    chans = padded.shape[3]
    total = jnp.zeros((count * height * width, weight.shape[2]), jnp.float32)
    for tap in range(9):
        row_off = tap // 3
        col_off = tap % 3
        window = padded[:, row_off : row_off + height, col_off : col_off + width, :].reshape(
            -1, chans
        )
        total = total + jnp.dot(window, weight[tap], preferred_element_type=jnp.float32)
    return total


def gathered_weights(state, probe_signs, timesteps, time_table, gn_gain, gn_shift, conv_weight, conv_bias):
    batch, tile_h, tile_w, chans = state.shape
    probes_here = probe_signs.shape[0]
    group_width = chans // GROUPS
    count = tile_h * lax.axis_size("gy") * tile_w * lax.axis_size("gx") * group_width
    xf = state.astype(jnp.float32)
    signs = probe_signs.astype(jnp.float32)
    grouped = xf.reshape(batch, tile_h, tile_w, GROUPS, group_width)
    signs_grouped = signs.reshape(probes_here, batch, tile_h, tile_w, GROUPS, group_width)
    sum_x = jnp.sum(grouped, axis=(1, 2, 4))
    sum_xx = jnp.sum(grouped * grouped, axis=(1, 2, 4))
    sum_u = jnp.sum(signs_grouped, axis=(2, 3, 5))
    cross = jnp.sum(signs_grouped * grouped[None], axis=(2, 3, 5))
    sum_x, sum_xx, sum_u, cross = lax.psum((sum_x, sum_xx, sum_u, cross), ("gy", "gx"))
    mean_x = sum_x / count
    centered = grouped - mean_x[:, None, None, :, None]
    sum_cu = cross - mean_x[None] * sum_u
    var_x = sum_xx / count - mean_x * mean_x
    sigma = jnp.sqrt(var_x + 1e-05)[:, None, None, :, None]
    normal = (centered / sigma).reshape(batch, tile_h, tile_w, chans)
    mean_u = (sum_u / count)[:, :, None, None, :, None]
    mean_cu = (sum_cu / count)[:, :, None, None, :, None]
    dnormal = (signs_grouped - mean_u) / sigma[None] - centered[None] * mean_cu / (
        sigma * sigma * sigma
    )[None]
    dnormal = dnormal.reshape(probes_here, batch, tile_h, tile_w, chans)
    onehot = (
        timesteps[:, None] == jnp.arange(time_table.shape[0], dtype=jnp.int32)[None, :]
    ).astype(jnp.float32)
    embed = jnp.dot(onehot, time_table, precision=lax.Precision.HIGHEST)
    pre = normal * gn_gain + gn_shift + embed[:, None, None, :]
    sig = jax.nn.sigmoid(pre)
    hidden = (pre * sig).astype(jnp.bfloat16)
    slope = sig * (1.0 + pre * (1.0 - sig)) * gn_gain
    dhidden = (slope[None] * dnormal).astype(jnp.bfloat16)
    flat_tangents = dhidden.reshape(probes_here * batch, tile_h, tile_w, chans)
    stacked = jnp.concatenate([hidden, flat_tangents], axis=0)
    items = stacked.shape[0]
    padded = with_halo(stacked, (("gy", 1), ("gx", 2)), 1)
    summed = local_conv(
        padded, lax.all_gather(conv_weight, "probe", axis=1, tiled=True), tile_h, tile_w
    )
    conv_out = summed.reshape(items, tile_h, tile_w, chans)
    conv_primal = conv_out[:batch]
    tangent = conv_out[batch:].reshape(probes_here, batch, tile_h, tile_w, chans)
    partial_sum = jnp.sum(signs * tangent, axis=(0, 2, 3, 4))
    velocity = conv_primal + conv_bias
    next_state = (xf + 0.25 * velocity).astype(jnp.bfloat16)
    total = lax.psum(partial_sum, ("gy", "gx", "probe"))
    logp_delta = -0.25 / (probes_here * lax.axis_size("probe")) * total
    return (next_state, logp_delta)


MESH = pl.DeviceIdType.MESH
F32 = jnp.float32
BF16 = jnp.bfloat16


def exact_dot(a, b):
    return jnp.dot(a, b, precision=lax.Precision.HIGHEST, preferred_element_type=F32)


def kernel(
    ny, nx, steps_ref, state_ref, signs_ref, time_hbm, gain_ref, shift_ref, bias_ref, w_hbm,
    out, l_out,
    time_ref, w_ref, state_f, halo, same, other, rest, acts, line, plane, vel, vel_in, parts,
    t_sem, w_sem, send, recv,
):
    gy, gx, me = lax.axis_index("gy"), lax.axis_index("gx"), lax.axis_index("probe")
    probes, batch, tile_h, tile_w, chans = signs_ref.shape
    rows = probes * batch
    share = w_ref.shape[1]
    cells = tile_h * tile_w
    width = chans // GROUPS
    count = cells * ny * nx * width
    w_copy = pltpu.make_async_copy(w_hbm, w_ref, w_sem)
    time_copy = pltpu.make_async_copy(time_hbm, time_ref, t_sem)
    time_copy.start()
    w_copy.start()

    def half(array, which):
        return jnp.where(which == 0, array, pltpu.roll(array, share, 1))[:, :share]

    def spots(step, size, landing):
        if step == 0:
            return pl.ds(1, size) if landing else pl.ds(0, size)
        if landing:
            return pl.ds(0, 1) if step > 0 else pl.ds(size + 1, 1)
        return pl.ds(size - 1, 1) if step > 0 else pl.ds(0, 1)

    def exists(dy, dx):
        y, x = gy + dy, gx + dx
        return (y >= 0) & (y < ny) & (x >= 0) & (x < nx)

    compass = [(dy, dx) for dy in (-1, 0, 1) for dx in (-1, 0, 1) if dy or dx]

    for slot in range(3):
        halo[slot] = jnp.zeros(halo.shape[1:], BF16)
    barrier = pltpu.get_barrier_semaphore()
    line_mates = [(gy, lax.rem(gx + k, nx), me) for k in range(1, nx)]
    plane_mates = [
        (lax.rem(gy + k, ny), gx, lax.rem(me + q, 2))
        for k in range(ny) for q in range(2) if k or q
    ]
    extra = [(dy, dx, q) for dy, dx in compass for q in range(2) if dx and (dy or q)]
    for mate in line_mates + plane_mates:
        pl.semaphore_signal(barrier, inc=1, device_id=mate, device_id_type=MESH)
    for dy, dx, q in extra:
        @pl.when(exists(dy, dx))
        def _():
            pl.semaphore_signal(
                barrier, inc=1, device_id=(gy + dy, gx + dx, lax.rem(me + q, 2)),
                device_id_type=MESH,
            )

    state_f[...] = state_ref[...].astype(F32)
    spot_list = [(y, w) for y in range(tile_h) for w in range(tile_w)]
    u = jnp.stack(
        [signs_ref[:, :, y, w, :].reshape(rows, chans) for y, w in spot_list]
    ).astype(F32)
    x = jnp.stack(
        [jnp.concatenate([state_f[:, y, w, :]] * probes, axis=0) for y, w in spot_list]
    )
    box = (tile_h, tile_w, rows, share)
    inner = (pl.ds(1, tile_h), pl.ds(1, tile_w))
    x_mine = half(x.reshape(cells * rows, chans), me).reshape(box).astype(BF16)
    u_flat = u.reshape(cells * rows, chans)
    u_mine = half(u_flat, me).reshape(box).astype(BF16)
    same[0] = x_mine
    same[1] = u_mine
    halo[(0,) + inner] = x_mine
    halo[(1,) + inner] = u_mine
    other[...] = half(u_flat, 1 - me).reshape(box).astype(BF16)
    sums = jnp.concatenate(
        [jnp.sum(x, 0), jnp.sum(x * x, 0), jnp.sum(u, 0), jnp.sum(u * x, 0)], axis=0
    )
    lanes = 128
    chan = lax.broadcasted_iota(jnp.int32, (chans, lanes), 0)
    group = lax.broadcasted_iota(jnp.int32, (chans, lanes), 1) * width
    pick = ((chan >= group) & (chan < group + width)).astype(F32)
    per_group = exact_dot(sums, pick)
    local = per_group[:rows]
    for k in range(1, 4):
        local = local + pltpu.roll(per_group[k * rows : (k + 1) * rows], GROUPS * k, 1)
    line[gx] = local

    greeted = len(line_mates) + len(plane_mates)
    for dy, dx, q in extra:
        greeted = greeted + jnp.where(exists(dy, dx), 1, 0)
    pl.semaphore_wait(barrier, greeted)

    taken = [0]

    def remote(src, dst, device):
        taken[0] += 1
        at = taken[0] - 1
        return pltpu.make_async_remote_copy(
            src_ref=src, dst_ref=dst, send_sem=send.at[at], recv_sem=recv.at[at],
            device_id=device, device_id_type=MESH,
        )

    def to_all(src, dst, mates):
        copies = [remote(src, dst, mate) for mate in mates]
        for copy in copies:
            copy.start()
        return copies

    line_copies = to_all(line.at[gx], line.at[gx], line_mates)
    tile_copy = remote(other, halo.at[(2,) + inner], (gy, gx, 1 - me))
    tile_copy.start()
    rims = []
    for dy, dx in compass:
        src = (spots(dy, tile_h, False), spots(dx, tile_w, False))
        dst = (spots(dy, tile_h, True), spots(dx, tile_w, True))
        both = [
            remote(
                same.at[(slice(None),) + src], halo.at[(pl.ds(0, 2),) + dst],
                (gy + dy, gx + dx, me),
            ),
            remote(other.at[src], halo.at[(2,) + dst], (gy + dy, gx + dx, 1 - me)),
        ]
        rims.append((dy, dx, both))

        @pl.when(exists(dy, dx))
        def _():
            for copy in both:
                copy.start()

    rest_copy = remote(same.at[1], rest, (gy, gx, 1 - me))
    rest_copy.start()

    for copy in line_copies:
        copy.wait()
    total = line[0]
    for k in range(1, nx):
        total = total + line[k]
    plane[gy, me] = total
    plane_copies = to_all(plane.at[gy, me], plane.at[gy, me], plane_mates)
    for copy in plane_copies:
        copy.wait()

    def moments(which):
        total = plane[0, which]
        for k in range(1, ny):
            total = total + plane[k, which]
        total = total / count
        valid = lax.broadcasted_iota(jnp.int32, total.shape, 1) < GROUPS
        return [
            jnp.where(valid, total if k == 0 else pltpu.roll(total, lanes - GROUPS * k, 1), 0.0)
            for k in range(4)
        ]

    mean_x, mean_xx, mean_u, cross = moments(me)
    _, _, mean_v, cross_v = moments(1 - me)
    inv = 1.0 / jnp.sqrt(mean_xx - mean_x * mean_x + 1e-05)
    cube = inv * inv * inv
    table = jnp.concatenate(
        [mean_x, inv, mean_u, (cross - mean_x * mean_u) * cube, mean_v,
         (cross_v - mean_x * mean_v) * cube], axis=0,
    )
    chan = lax.broadcasted_iota(jnp.int32, (lanes, share), 1) + me * share
    group = lax.broadcasted_iota(jnp.int32, (lanes, share), 0) * width
    spread = ((chan >= group) & (chan < group + width)).astype(F32)
    table = exact_dot(table, spread)
    mean_x, inv, mean_u, mean_cu, mean_v, mean_cv = [
        table[k * rows : (k + 1) * rows] for k in range(6)
    ]
    time_copy.wait()
    embed = jnp.concatenate(
        [time_ref[pl.ds(steps_ref[b], 1), :] for b in range(batch)] * probes, axis=0
    )
    offset = half(embed + shift_ref[...].reshape(1, chans), me)
    gain = half(jnp.broadcast_to(gain_ref[...].reshape(1, chans), (rows, chans)), me)

    tile_copy.wait()
    for dy, dx, both in rims:
        @pl.when(exists(dy, dx))
        def _():
            for copy in both:
                copy.wait_send()

        @pl.when(exists(-dy, -dx))
        def _():
            for copy in both:
                copy.wait_recv()

    for y in range(tile_h + 2):
        centered = halo[0, y].astype(F32) - mean_x
        normal = centered * inv
        pre = normal * gain + offset
        sig = 1.0 / (1.0 + jnp.exp(-pre))
        slope = sig * (1.0 + pre * (1.0 - sig)) * gain
        acts[y, :, 0:rows] = pre * sig
        acts[y, :, rows : 2 * rows] = slope * (
            (halo[1, y].astype(F32) - mean_u) * inv - centered * mean_cu
        )
        acts[y, :, 2 * rows :] = slope * (
            (halo[2, y].astype(F32) - mean_v) * inv - centered * mean_cv
        )
    for edge, at in (
        (gy == 0, (0,)), (gy == ny - 1, (tile_h + 1,)),
        (gx == 0, (slice(None), 0)), (gx == nx - 1, (slice(None), tile_w + 1)),
    ):
        @pl.when(edge)
        def _():
            acts[at] = jnp.zeros(acts.at[at].shape, F32)

    def conv(first, size):
        total = None
        for tap in range(9):
            dy, dx = tap // 3, tap % 3
            window = acts[dy : dy + tile_h, dx : dx + tile_w, first : first + size]
            window = window.reshape(cells * size, share).astype(BF16)
            part = jnp.dot(window, w_ref[tap], preferred_element_type=F32)
            total = part if total is None else total + part
        return total.reshape(cells, size, chans)

    w_copy.wait()
    vel[...] = conv(0, rows)[:, :batch]
    vel_copy = remote(vel, vel_in, (gy, gx, 1 - me))
    vel_copy.start()
    tangent = conv(rows, 2 * rows).reshape(cells * 2 * rows, chans)
    rest_copy.wait()

    def pairs(at):
        return at.astype(F32).reshape(cells, rows, share)

    near = half(tangent, me).reshape(cells, 2 * rows, share)
    far = half(tangent, 1 - me).reshape(cells, 2 * rows, share)
    product = jnp.sum(
        pairs(same[1]) * near[:, :rows] + pairs(halo[(2,) + inner]) * near[:, rows:]
        + pairs(other[...]) * far[:, :rows] + pairs(rest[...]) * far[:, rows:],
        axis=0,
    )
    product = jnp.sum(product, axis=1, keepdims=True)
    lane = lax.broadcasted_iota(jnp.int32, (rows, lanes), 1)
    row = lax.broadcasted_iota(jnp.int32, (rows, lanes), 0)
    here = jnp.where(lane == lax.rem(row, batch), product, 0.0)
    mine = (gy * nx + gx) * 2 + me
    parts[mine] = jnp.sum(here, axis=0, keepdims=True)
    everyone = [
        (lax.rem(gy + a, ny), lax.rem(gx + b, nx), lax.rem(me + q, 2))
        for a in range(ny) for b in range(nx) for q in range(2) if a or b or q
    ]
    copies = to_all(parts.at[mine], parts.at[mine], everyone)
    vel_copy.wait()
    vel[...] = 0.25 * (vel[...] + vel_in[...] + bias_ref[...].reshape(1, chans))
    for b in range(batch):
        for y in range(tile_h):
            moved = vel[y * tile_w : (y + 1) * tile_w, b, :]
            out[b, y] = (state_f[b, y] + moved).astype(BF16)
    for copy in copies:
        copy.wait()
    l_out[...] = jnp.sum(parts[...], axis=0) * (-0.25 / (2 * probes))


def one_kernel(state, probe_signs, timesteps, time_table, gn_gain, gn_shift, conv_weight, conv_bias):
    batch, tile_h, tile_w, chans = state.shape
    probes = probe_signs.shape[0]
    share = conv_weight.shape[1]
    ny, nx = lax.axis_size("gy"), lax.axis_size("gx")
    rows = probes * batch
    cells = tile_h * tile_w
    copies = (nx - 1) + (2 * ny - 1) + 3 + 16 + (2 * nx * ny - 1)
    vmem = pl.BlockSpec(memory_space=pltpu.VMEM)
    hbm = pl.BlockSpec(memory_space=pl.ANY)
    next_state, total = pl.pallas_call(
        functools.partial(kernel, ny, nx),
        out_shape=(
            jax.ShapeDtypeStruct(state.shape, BF16),
            jax.ShapeDtypeStruct((1, 128), F32),
        ),
        in_specs=[
            pl.BlockSpec(memory_space=pltpu.SMEM), vmem, vmem, hbm, vmem, vmem, vmem, hbm
        ],
        out_specs=(vmem, vmem),
        scratch_shapes=[
            pltpu.VMEM(time_table.shape, F32),
            pltpu.VMEM(conv_weight.shape, BF16),
            pltpu.VMEM(state.shape, F32),
            pltpu.VMEM((3, tile_h + 2, tile_w + 2, rows, share), BF16),
            pltpu.VMEM((2, tile_h, tile_w, rows, share), BF16),
            pltpu.VMEM((tile_h, tile_w, rows, share), BF16),
            pltpu.VMEM((tile_h, tile_w, rows, share), BF16),
            pltpu.VMEM((tile_h + 2, tile_w + 2, 3 * rows, share), F32),
            pltpu.VMEM((nx, rows, 128), F32),
            pltpu.VMEM((ny, 2, rows, 128), F32),
            pltpu.VMEM((cells, batch, chans), F32),
            pltpu.VMEM((cells, batch, chans), F32),
            pltpu.VMEM((2 * nx * ny, 1, 128), F32),
            pltpu.SemaphoreType.DMA,
            pltpu.SemaphoreType.DMA,
            pltpu.SemaphoreType.DMA((copies,)),
            pltpu.SemaphoreType.DMA((copies,)),
        ],
        compiler_params=pltpu.CompilerParams(collective_id=0, has_side_effects=True),
    )(
        timesteps, state, probe_signs, time_table, gn_gain,
        gn_shift, conv_bias, conv_weight,
    )
    return (next_state, total[0, :batch])


def solution(mesh):
    def body(*args):
        wide = mesh.shape["probe"] == 2 and args[6].shape[1] >= 128
        rows = args[1].shape[0] * args[0].shape[0]
        return (one_kernel if wide and rows == 8 else gathered_weights)(*args)

    in_specs = (
        P(None, "gy", "gx", None),
        P("probe", None, "gy", "gx", None),
        P(),
        P(),
        P(),
        P(),
        P(None, "probe", None),
        P(),
    )
    out_specs = (P(None, "gy", "gx", None), P())
    return jax.shard_map(body, mesh=mesh, in_specs=in_specs, out_specs=out_specs, check_vma=False)
```

```python
import functools

import jax
import jax.numpy as jnp
from jax import lax
from jax.experimental import pallas as pl
from jax.experimental.pallas import tpu as pltpu
from jax.sharding import PartitionSpec as P

GROUPS = 32


def with_halo(block, sides, width):
    for axis, dim in sides:
        count = lax.axis_size(axis)
        forward = [(i, i + 1) for i in range(count - 1)]
        backward = [(target, source) for source, target in forward]
        low = lax.ppermute(
            lax.slice_in_dim(block, block.shape[dim] - width, None, axis=dim), axis, forward
        )
        high = lax.ppermute(lax.slice_in_dim(block, 0, width, axis=dim), axis, backward)
        block = jnp.concatenate([low, block, high], axis=dim)
    return block


def local_conv(padded, weight, height, width):
    count = padded.shape[0]
    chans = padded.shape[3]
    total = jnp.zeros((count * height * width, weight.shape[2]), jnp.float32)
    for tap in range(9):
        row_off = tap // 3
        col_off = tap % 3
        window = padded[:, row_off : row_off + height, col_off : col_off + width, :].reshape(
            -1, chans
        )
        total = total + jnp.dot(window, weight[tap], preferred_element_type=jnp.float32)
    return total


def gathered_weights(state, probe_signs, timesteps, time_table, gn_gain, gn_shift, conv_weight, conv_bias):
    batch, tile_h, tile_w, chans = state.shape
    probes_here = probe_signs.shape[0]
    group_width = chans // GROUPS
    count = tile_h * lax.axis_size("gy") * tile_w * lax.axis_size("gx") * group_width
    xf = state.astype(jnp.float32)
    signs = probe_signs.astype(jnp.float32)
    grouped = xf.reshape(batch, tile_h, tile_w, GROUPS, group_width)
    signs_grouped = signs.reshape(probes_here, batch, tile_h, tile_w, GROUPS, group_width)
    sum_x = jnp.sum(grouped, axis=(1, 2, 4))
    sum_xx = jnp.sum(grouped * grouped, axis=(1, 2, 4))
    sum_u = jnp.sum(signs_grouped, axis=(2, 3, 5))
    cross = jnp.sum(signs_grouped * grouped[None], axis=(2, 3, 5))
    sum_x, sum_xx, sum_u, cross = lax.psum((sum_x, sum_xx, sum_u, cross), ("gy", "gx"))
    mean_x = sum_x / count
    centered = grouped - mean_x[:, None, None, :, None]
    sum_cu = cross - mean_x[None] * sum_u
    var_x = sum_xx / count - mean_x * mean_x
    sigma = jnp.sqrt(var_x + 1e-05)[:, None, None, :, None]
    normal = (centered / sigma).reshape(batch, tile_h, tile_w, chans)
    mean_u = (sum_u / count)[:, :, None, None, :, None]
    mean_cu = (sum_cu / count)[:, :, None, None, :, None]
    dnormal = (signs_grouped - mean_u) / sigma[None] - centered[None] * mean_cu / (
        sigma * sigma * sigma
    )[None]
    dnormal = dnormal.reshape(probes_here, batch, tile_h, tile_w, chans)
    onehot = (
        timesteps[:, None] == jnp.arange(time_table.shape[0], dtype=jnp.int32)[None, :]
    ).astype(jnp.float32)
    embed = jnp.dot(onehot, time_table, precision=lax.Precision.HIGHEST)
    pre = normal * gn_gain + gn_shift + embed[:, None, None, :]
    sig = jax.nn.sigmoid(pre)
    hidden = (pre * sig).astype(jnp.bfloat16)
    slope = sig * (1.0 + pre * (1.0 - sig)) * gn_gain
    dhidden = (slope[None] * dnormal).astype(jnp.bfloat16)
    flat_tangents = dhidden.reshape(probes_here * batch, tile_h, tile_w, chans)
    stacked = jnp.concatenate([hidden, flat_tangents], axis=0)
    items = stacked.shape[0]
    padded = with_halo(stacked, (("gy", 1), ("gx", 2)), 1)
    summed = local_conv(
        padded, lax.all_gather(conv_weight, "probe", axis=1, tiled=True), tile_h, tile_w
    )
    conv_out = summed.reshape(items, tile_h, tile_w, chans)
    conv_primal = conv_out[:batch]
    tangent = conv_out[batch:].reshape(probes_here, batch, tile_h, tile_w, chans)
    partial_sum = jnp.sum(signs * tangent, axis=(0, 2, 3, 4))
    velocity = conv_primal + conv_bias
    next_state = (xf + 0.25 * velocity).astype(jnp.bfloat16)
    total = lax.psum(partial_sum, ("gy", "gx", "probe"))
    logp_delta = -0.25 / (probes_here * lax.axis_size("probe")) * total
    return (next_state, logp_delta)


MESH = pl.DeviceIdType.MESH
F32 = jnp.float32
BF16 = jnp.bfloat16


def exact_dot(a, b):
    return jnp.dot(a, b, precision=lax.Precision.HIGHEST, preferred_element_type=F32)


def kernel(
    ny, nx, steps_ref, state_hbm, signs_hbm, time_hbm, gain_hbm, shift_hbm, bias_hbm, w_hbm,
    out, l_out,
    state_ref, signs_ref, time_ref, gain_ref, shift_ref, bias_ref, w_ref, state_f, halo, same, other, rest, acts, line, plane, vel, vel_in, parts,
    fetched, send, recv,
):
    gy, gx, me = lax.axis_index("gy"), lax.axis_index("gx"), lax.axis_index("probe")
    probes, batch, tile_h, tile_w, chans = signs_ref.shape
    rows = probes * batch
    share = w_ref.shape[1]
    cells = tile_h * tile_w
    width = chans // GROUPS
    count = cells * ny * nx * width
    inputs = [
        pltpu.make_async_copy(src, dst, fetched.at[at])
        for at, (src, dst) in enumerate([
            (state_hbm, state_ref), (signs_hbm, signs_ref), (time_hbm, time_ref),
            (gain_hbm, gain_ref), (shift_hbm, shift_ref), (bias_hbm, bias_ref), (w_hbm, w_ref),
        ])
    ]

    def half(array, which):
        return jnp.where(which == 0, array, pltpu.roll(array, share, 1))[:, :share]

    def spots(step, size, landing):
        if step == 0:
            return pl.ds(1, size) if landing else pl.ds(0, size)
        if landing:
            return pl.ds(0, 1) if step > 0 else pl.ds(size + 1, 1)
        return pl.ds(size - 1, 1) if step > 0 else pl.ds(0, 1)

    def exists(dy, dx):
        y, x = gy + dy, gx + dx
        return (y >= 0) & (y < ny) & (x >= 0) & (x < nx)

    compass = [(dy, dx) for dy in (-1, 0, 1) for dx in (-1, 0, 1) if dy or dx]

    barrier = pltpu.get_barrier_semaphore()
    line_mates = [(gy, lax.rem(gx + k, nx), me) for k in range(1, nx)]
    plane_mates = [
        (lax.rem(gy + k, ny), gx, lax.rem(me + q, 2))
        for k in range(ny) for q in range(2) if k or q
    ]
    extra = [(dy, dx, q) for dy, dx in compass for q in range(2) if dx and (dy or q)]
    for mate in line_mates + plane_mates:
        pl.semaphore_signal(barrier, inc=1, device_id=mate, device_id_type=MESH)
    for dy, dx, q in extra:
        @pl.when(exists(dy, dx))
        def _():
            pl.semaphore_signal(
                barrier, inc=1, device_id=(gy + dy, gx + dx, lax.rem(me + q, 2)),
                device_id_type=MESH,
            )

    for copy in inputs:
        copy.start()

    inputs[0].wait()
    inputs[1].wait()
    state_f[...] = state_ref[...].astype(F32)
    spot_list = [(y, w) for y in range(tile_h) for w in range(tile_w)]
    u = jnp.stack(
        [signs_ref[:, :, y, w, :].reshape(rows, chans) for y, w in spot_list]
    ).astype(F32)
    x = jnp.stack(
        [jnp.concatenate([state_f[:, y, w, :]] * probes, axis=0) for y, w in spot_list]
    )
    box = (tile_h, tile_w, rows, share)
    inner = (pl.ds(1, tile_h), pl.ds(1, tile_w))
    x_mine = half(x.reshape(cells * rows, chans), me).reshape(box).astype(BF16)
    u_flat = u.reshape(cells * rows, chans)
    u_mine = half(u_flat, me).reshape(box).astype(BF16)
    same[0] = x_mine
    same[1] = u_mine
    halo[(0,) + inner] = x_mine
    halo[(1,) + inner] = u_mine
    other[...] = half(u_flat, 1 - me).reshape(box).astype(BF16)
    sums = jnp.concatenate(
        [jnp.sum(x, 0), jnp.sum(x * x, 0), jnp.sum(u, 0), jnp.sum(u * x, 0)], axis=0
    )
    lanes = 128
    chan = lax.broadcasted_iota(jnp.int32, (chans, lanes), 0)
    group = lax.broadcasted_iota(jnp.int32, (chans, lanes), 1) * width
    pick = ((chan >= group) & (chan < group + width)).astype(F32)
    per_group = exact_dot(sums, pick)
    local = per_group[:rows]
    for k in range(1, 4):
        local = local + pltpu.roll(per_group[k * rows : (k + 1) * rows], GROUPS * k, 1)
    plane[gy, me] = local

    greeted = len(line_mates) + len(plane_mates)
    for dy, dx, q in extra:
        greeted = greeted + jnp.where(exists(dy, dx), 1, 0)
    pl.semaphore_wait(barrier, greeted)

    taken = [0]

    def remote(src, dst, device):
        taken[0] += 1
        at = taken[0] - 1
        return pltpu.make_async_remote_copy(
            src_ref=src, dst_ref=dst, send_sem=send.at[at], recv_sem=recv.at[at],
            device_id=device, device_id_type=MESH,
        )

    def to_all(src, dst, mates):
        copies = [remote(src, dst, mate) for mate in mates]
        for copy in copies:
            copy.start()
        return copies

    plane_copies = to_all(plane.at[gy, me], plane.at[gy, me], plane_mates)
    tile_copy = remote(other, halo.at[(2,) + inner], (gy, gx, 1 - me))
    tile_copy.start()
    rims = []
    for dy, dx in compass:
        src = (spots(dy, tile_h, False), spots(dx, tile_w, False))
        dst = (spots(dy, tile_h, True), spots(dx, tile_w, True))
        both = [
            remote(
                same.at[(slice(None),) + src], halo.at[(pl.ds(0, 2),) + dst],
                (gy + dy, gx + dx, me),
            ),
            remote(other.at[src], halo.at[(2,) + dst], (gy + dy, gx + dx, 1 - me)),
        ]
        rims.append((dy, dx, both))

        @pl.when(exists(dy, dx))
        def _():
            for copy in both:
                copy.start()

    for copy in plane_copies:
        copy.wait()
    for which in range(2):
        total = plane[0, which]
        for k in range(1, ny):
            total = total + plane[k, which]
        line[gx, which] = total
    line_copies = to_all(line.at[gx], line.at[gx], line_mates)
    rest_copy = remote(same.at[1], rest, (gy, gx, 1 - me))
    rest_copy.start()
    for copy in line_copies:
        copy.wait()

    def moments(which):
        total = line[0, which]
        for k in range(1, nx):
            total = total + line[k, which]
        total = total / count
        valid = lax.broadcasted_iota(jnp.int32, total.shape, 1) < GROUPS
        return [
            jnp.where(valid, total if k == 0 else pltpu.roll(total, lanes - GROUPS * k, 1), 0.0)
            for k in range(4)
        ]

    mean_x, mean_xx, mean_u, cross = moments(me)
    _, _, mean_v, cross_v = moments(1 - me)
    inv = 1.0 / jnp.sqrt(mean_xx - mean_x * mean_x + 1e-05)
    cube = inv * inv * inv
    table = jnp.concatenate(
        [mean_x, inv, mean_u, (cross - mean_x * mean_u) * cube, mean_v,
         (cross_v - mean_x * mean_v) * cube], axis=0,
    )
    chan = lax.broadcasted_iota(jnp.int32, (lanes, share), 1) + me * share
    group = lax.broadcasted_iota(jnp.int32, (lanes, share), 0) * width
    spread = ((chan >= group) & (chan < group + width)).astype(F32)
    table = exact_dot(table, spread)
    mean_x, inv, mean_u, mean_cu, mean_v, mean_cv = [
        table[k * rows : (k + 1) * rows] for k in range(6)
    ]
    for copy in inputs[2:6]:
        copy.wait()
    embed = jnp.concatenate(
        [time_ref[pl.ds(steps_ref[b], 1), :] for b in range(batch)] * probes, axis=0
    )
    offset = half(embed + shift_ref[...].reshape(1, chans), me)
    gain = half(jnp.broadcast_to(gain_ref[...].reshape(1, chans), (rows, chans)), me)

    tile_copy.wait()
    for dy, dx, both in rims:
        @pl.when(exists(dy, dx))
        def _():
            for copy in both:
                copy.wait_send()

        @pl.when(exists(-dy, -dx))
        def _():
            for copy in both:
                copy.wait_recv()

    for y in range(tile_h + 2):
        centered = halo[0, y].astype(F32) - mean_x
        normal = centered * inv
        pre = normal * gain + offset
        sig = 1.0 / (1.0 + jnp.exp(-pre))
        slope = sig * (1.0 + pre * (1.0 - sig)) * gain
        acts[y, :, 0:rows] = pre * sig
        acts[y, :, rows : 2 * rows] = slope * (
            (halo[1, y].astype(F32) - mean_u) * inv - centered * mean_cu
        )
        acts[y, :, 2 * rows :] = slope * (
            (halo[2, y].astype(F32) - mean_v) * inv - centered * mean_cv
        )
    for edge, at in (
        (gy == 0, (0,)), (gy == ny - 1, (tile_h + 1,)),
        (gx == 0, (slice(None), 0)), (gx == nx - 1, (slice(None), tile_w + 1)),
    ):
        @pl.when(edge)
        def _():
            acts[at] = jnp.zeros(acts.at[at].shape, F32)

    def conv(first, size):
        total = None
        for tap in range(9):
            dy, dx = tap // 3, tap % 3
            window = acts[dy : dy + tile_h, dx : dx + tile_w, first : first + size]
            window = window.reshape(cells * size, share).astype(BF16)
            part = jnp.dot(window, w_ref[tap], preferred_element_type=F32)
            total = part if total is None else total + part
        return total.reshape(cells, size, chans)

    inputs[6].wait()
    vel[...] = conv(0, rows)[:, :batch]
    vel_copy = remote(vel, vel_in, (gy, gx, 1 - me))
    vel_copy.start()
    tangent = conv(rows, 2 * rows).reshape(cells * 2 * rows, chans)
    rest_copy.wait()

    def pairs(at):
        return at.astype(F32).reshape(cells, rows, share)

    near = half(tangent, me).reshape(cells, 2 * rows, share)
    far = half(tangent, 1 - me).reshape(cells, 2 * rows, share)
    product = jnp.sum(
        pairs(same[1]) * near[:, :rows] + pairs(halo[(2,) + inner]) * near[:, rows:]
        + pairs(other[...]) * far[:, :rows] + pairs(rest[...]) * far[:, rows:],
        axis=0,
    )
    product = jnp.sum(product, axis=1, keepdims=True)
    lane = lax.broadcasted_iota(jnp.int32, (rows, lanes), 1)
    row = lax.broadcasted_iota(jnp.int32, (rows, lanes), 0)
    here = jnp.where(lane == lax.rem(row, batch), product, 0.0)
    mine = (gy * nx + gx) * 2 + me
    parts[mine] = jnp.sum(here, axis=0, keepdims=True)
    everyone = [
        (lax.rem(gy + a, ny), lax.rem(gx + b, nx), lax.rem(me + q, 2))
        for a in range(ny) for b in range(nx) for q in range(2) if a or b or q
    ]
    copies = to_all(parts.at[mine], parts.at[mine], everyone)
    vel_copy.wait()
    vel[...] = 0.25 * (vel[...] + vel_in[...] + bias_ref[...].reshape(1, chans))
    for b in range(batch):
        for y in range(tile_h):
            moved = vel[y * tile_w : (y + 1) * tile_w, b, :]
            out[b, y] = (state_f[b, y] + moved).astype(BF16)
    for copy in copies:
        copy.wait()
    l_out[...] = jnp.sum(parts[...], axis=0) * (-0.25 / (2 * probes))


def one_kernel(state, probe_signs, timesteps, time_table, gn_gain, gn_shift, conv_weight, conv_bias):
    batch, tile_h, tile_w, chans = state.shape
    probes = probe_signs.shape[0]
    share = conv_weight.shape[1]
    ny, nx = lax.axis_size("gy"), lax.axis_size("gx")
    rows = probes * batch
    cells = tile_h * tile_w
    copies = (nx - 1) + (2 * ny - 1) + 3 + 16 + (2 * nx * ny - 1)
    vmem = pl.BlockSpec(memory_space=pltpu.VMEM)
    hbm = pl.BlockSpec(memory_space=pl.ANY)
    next_state, total = pl.pallas_call(
        functools.partial(kernel, ny, nx),
        out_shape=(
            jax.ShapeDtypeStruct(state.shape, BF16),
            jax.ShapeDtypeStruct((1, 128), F32),
        ),
        in_specs=[pl.BlockSpec(memory_space=pltpu.SMEM)] + [hbm] * 7,
        out_specs=(vmem, vmem),
        scratch_shapes=[
            pltpu.VMEM(state.shape, BF16),
            pltpu.VMEM(probe_signs.shape, jnp.int32),
            pltpu.VMEM(time_table.shape, F32),
            pltpu.VMEM(gn_gain.shape, F32),
            pltpu.VMEM(gn_shift.shape, F32),
            pltpu.VMEM(conv_bias.shape, F32),
            pltpu.VMEM(conv_weight.shape, BF16),
            pltpu.VMEM(state.shape, F32),
            pltpu.VMEM((3, tile_h + 2, tile_w + 2, rows, share), BF16),
            pltpu.VMEM((2, tile_h, tile_w, rows, share), BF16),
            pltpu.VMEM((tile_h, tile_w, rows, share), BF16),
            pltpu.VMEM((tile_h, tile_w, rows, share), BF16),
            pltpu.VMEM((tile_h + 2, tile_w + 2, 3 * rows, share), F32),
            pltpu.VMEM((nx, 2, rows, 128), F32),
            pltpu.VMEM((ny, 2, rows, 128), F32),
            pltpu.VMEM((cells, batch, chans), F32),
            pltpu.VMEM((cells, batch, chans), F32),
            pltpu.VMEM((2 * nx * ny, 1, 128), F32),
            pltpu.SemaphoreType.DMA((7,)),
            pltpu.SemaphoreType.DMA((copies,)),
            pltpu.SemaphoreType.DMA((copies,)),
        ],
        compiler_params=pltpu.CompilerParams(collective_id=0, has_side_effects=True),
    )(
        timesteps, state, probe_signs, time_table, gn_gain,
        gn_shift, conv_bias, conv_weight,
    )
    return (next_state, total[0, :batch])


def solution(mesh):
    def body(*args):
        wide = mesh.shape["probe"] == 2 and args[6].shape[1] >= 128
        rows = args[1].shape[0] * args[0].shape[0]
        return (one_kernel if wide and rows == 8 else gathered_weights)(*args)

    in_specs = (
        P(None, "gy", "gx", None),
        P("probe", None, "gy", "gx", None),
        P(),
        P(),
        P(),
        P(),
        P(None, "probe", None),
        P(),
    )
    out_specs = (P(None, "gy", "gx", None), P())
    return jax.shard_map(body, mesh=mesh, in_specs=in_specs, out_specs=out_specs, check_vma=False)
```

```python
import functools

import jax
import jax.numpy as jnp
from jax import lax
from jax.experimental import pallas as pl
from jax.experimental.pallas import tpu as pltpu
from jax.sharding import PartitionSpec as P

GROUPS = 32


def with_halo(block, sides, width):
    for axis, dim in sides:
        count = lax.axis_size(axis)
        forward = [(i, i + 1) for i in range(count - 1)]
        backward = [(target, source) for source, target in forward]
        low = lax.ppermute(
            lax.slice_in_dim(block, block.shape[dim] - width, None, axis=dim), axis, forward
        )
        high = lax.ppermute(lax.slice_in_dim(block, 0, width, axis=dim), axis, backward)
        block = jnp.concatenate([low, block, high], axis=dim)
    return block


def local_conv(padded, weight, height, width):
    count = padded.shape[0]
    chans = padded.shape[3]
    total = jnp.zeros((count * height * width, weight.shape[2]), jnp.float32)
    for tap in range(9):
        row_off = tap // 3
        col_off = tap % 3
        window = padded[:, row_off : row_off + height, col_off : col_off + width, :].reshape(
            -1, chans
        )
        total = total + jnp.dot(window, weight[tap], preferred_element_type=jnp.float32)
    return total


def gathered_weights(state, probe_signs, timesteps, time_table, gn_gain, gn_shift, conv_weight, conv_bias):
    batch, tile_h, tile_w, chans = state.shape
    probes_here = probe_signs.shape[0]
    group_width = chans // GROUPS
    count = tile_h * lax.axis_size("gy") * tile_w * lax.axis_size("gx") * group_width
    xf = state.astype(jnp.float32)
    signs = probe_signs.astype(jnp.float32)
    grouped = xf.reshape(batch, tile_h, tile_w, GROUPS, group_width)
    signs_grouped = signs.reshape(probes_here, batch, tile_h, tile_w, GROUPS, group_width)
    sum_x = jnp.sum(grouped, axis=(1, 2, 4))
    sum_xx = jnp.sum(grouped * grouped, axis=(1, 2, 4))
    sum_u = jnp.sum(signs_grouped, axis=(2, 3, 5))
    cross = jnp.sum(signs_grouped * grouped[None], axis=(2, 3, 5))
    sum_x, sum_xx, sum_u, cross = lax.psum((sum_x, sum_xx, sum_u, cross), ("gy", "gx"))
    mean_x = sum_x / count
    centered = grouped - mean_x[:, None, None, :, None]
    sum_cu = cross - mean_x[None] * sum_u
    var_x = sum_xx / count - mean_x * mean_x
    sigma = jnp.sqrt(var_x + 1e-05)[:, None, None, :, None]
    normal = (centered / sigma).reshape(batch, tile_h, tile_w, chans)
    mean_u = (sum_u / count)[:, :, None, None, :, None]
    mean_cu = (sum_cu / count)[:, :, None, None, :, None]
    dnormal = (signs_grouped - mean_u) / sigma[None] - centered[None] * mean_cu / (
        sigma * sigma * sigma
    )[None]
    dnormal = dnormal.reshape(probes_here, batch, tile_h, tile_w, chans)
    onehot = (
        timesteps[:, None] == jnp.arange(time_table.shape[0], dtype=jnp.int32)[None, :]
    ).astype(jnp.float32)
    embed = jnp.dot(onehot, time_table, precision=lax.Precision.HIGHEST)
    pre = normal * gn_gain + gn_shift + embed[:, None, None, :]
    sig = jax.nn.sigmoid(pre)
    hidden = (pre * sig).astype(jnp.bfloat16)
    slope = sig * (1.0 + pre * (1.0 - sig)) * gn_gain
    dhidden = (slope[None] * dnormal).astype(jnp.bfloat16)
    flat_tangents = dhidden.reshape(probes_here * batch, tile_h, tile_w, chans)
    stacked = jnp.concatenate([hidden, flat_tangents], axis=0)
    items = stacked.shape[0]
    padded = with_halo(stacked, (("gy", 1), ("gx", 2)), 1)
    summed = local_conv(
        padded, lax.all_gather(conv_weight, "probe", axis=1, tiled=True), tile_h, tile_w
    )
    conv_out = summed.reshape(items, tile_h, tile_w, chans)
    conv_primal = conv_out[:batch]
    tangent = conv_out[batch:].reshape(probes_here, batch, tile_h, tile_w, chans)
    partial_sum = jnp.sum(signs * tangent, axis=(0, 2, 3, 4))
    velocity = conv_primal + conv_bias
    next_state = (xf + 0.25 * velocity).astype(jnp.bfloat16)
    total = lax.psum(partial_sum, ("gy", "gx", "probe"))
    logp_delta = -0.25 / (probes_here * lax.axis_size("probe")) * total
    return (next_state, logp_delta)


MESH = pl.DeviceIdType.MESH
F32 = jnp.float32
BF16 = jnp.bfloat16


def exact_dot(a, b):
    return jnp.dot(a, b, precision=lax.Precision.HIGHEST, preferred_element_type=F32)


def kernel(
    ny, nx, steps_ref, state_hbm, signs_hbm, time_hbm, gain_hbm, shift_hbm, bias_hbm, w_hbm,
    out, l_out,
    state_ref, signs_ref, time_ref, gain_ref, shift_ref, bias_ref, w_ref, state_f, halo, same, other, rest, acts, cols, line, plane, vel, vel_in, parts,
    fetched, send, recv,
):
    gy, gx, me = lax.axis_index("gy"), lax.axis_index("gx"), lax.axis_index("probe")
    probes, batch, tile_h, tile_w, chans = signs_ref.shape
    rows = probes * batch
    share = w_ref.shape[0] // 9
    cells = tile_h * tile_w
    width = chans // GROUPS
    count = cells * ny * nx * width
    inputs = [
        pltpu.make_async_copy(src, dst, fetched.at[at])
        for at, (src, dst) in enumerate([
            (state_hbm, state_ref), (signs_hbm, signs_ref), (time_hbm, time_ref),
            (gain_hbm, gain_ref), (shift_hbm, shift_ref), (bias_hbm, bias_ref), (w_hbm, w_ref),
        ])
    ]

    def half(array, which):
        return jnp.where(which == 0, array, pltpu.roll(array, share, 1))[:, :share]

    def spots(step, size, landing):
        if step == 0:
            return pl.ds(1, size) if landing else pl.ds(0, size)
        if landing:
            return pl.ds(0, 1) if step > 0 else pl.ds(size + 1, 1)
        return pl.ds(size - 1, 1) if step > 0 else pl.ds(0, 1)

    def exists(dy, dx):
        y, x = gy + dy, gx + dx
        return (y >= 0) & (y < ny) & (x >= 0) & (x < nx)

    compass = [(dy, dx) for dy in (-1, 0, 1) for dx in (-1, 0, 1) if dy or dx]

    barrier = pltpu.get_barrier_semaphore()
    line_mates = [(gy, lax.rem(gx + k, nx), me) for k in range(1, nx)]
    plane_mates = [
        (lax.rem(gy + k, ny), gx, lax.rem(me + q, 2))
        for k in range(ny) for q in range(2) if k or q
    ]
    extra = [(dy, dx, q) for dy, dx in compass for q in range(2) if dx and (dy or q)]
    for mate in line_mates + plane_mates:
        pl.semaphore_signal(barrier, inc=1, device_id=mate, device_id_type=MESH)
    for dy, dx, q in extra:
        @pl.when(exists(dy, dx))
        def _():
            pl.semaphore_signal(
                barrier, inc=1, device_id=(gy + dy, gx + dx, lax.rem(me + q, 2)),
                device_id_type=MESH,
            )

    for copy in inputs:
        copy.start()

    inputs[0].wait()
    inputs[1].wait()
    state_f[...] = state_ref[...].astype(F32)
    spot_list = [(y, w) for y in range(tile_h) for w in range(tile_w)]
    u = jnp.stack(
        [signs_ref[:, :, y, w, :].reshape(rows, chans) for y, w in spot_list]
    ).astype(F32)
    x = jnp.stack(
        [jnp.concatenate([state_f[:, y, w, :]] * probes, axis=0) for y, w in spot_list]
    )
    box = (tile_h, tile_w, rows, share)
    inner = (pl.ds(1, tile_h), pl.ds(1, tile_w))
    x_mine = half(x.reshape(cells * rows, chans), me).reshape(box).astype(BF16)
    u_flat = u.reshape(cells * rows, chans)
    u_mine = half(u_flat, me).reshape(box).astype(BF16)
    same[0] = x_mine
    same[1] = u_mine
    halo[(0,) + inner] = x_mine
    halo[(1,) + inner] = u_mine
    other[...] = half(u_flat, 1 - me).reshape(box).astype(BF16)
    sums = jnp.concatenate(
        [jnp.sum(x, 0), jnp.sum(x * x, 0), jnp.sum(u, 0), jnp.sum(u * x, 0)], axis=0
    )
    lanes = 128
    chan = lax.broadcasted_iota(jnp.int32, (chans, lanes), 0)
    group = lax.broadcasted_iota(jnp.int32, (chans, lanes), 1) * width
    pick = ((chan >= group) & (chan < group + width)).astype(F32)
    per_group = exact_dot(sums, pick)
    local = per_group[:rows]
    for k in range(1, 4):
        local = local + pltpu.roll(per_group[k * rows : (k + 1) * rows], GROUPS * k, 1)
    plane[gy, me] = local

    greeted = len(line_mates) + len(plane_mates)
    for dy, dx, q in extra:
        greeted = greeted + jnp.where(exists(dy, dx), 1, 0)
    pl.semaphore_wait(barrier, greeted)

    taken = [0]

    def remote(src, dst, device):
        taken[0] += 1
        at = taken[0] - 1
        return pltpu.make_async_remote_copy(
            src_ref=src, dst_ref=dst, send_sem=send.at[at], recv_sem=recv.at[at],
            device_id=device, device_id_type=MESH,
        )

    def to_all(src, dst, mates):
        copies = [remote(src, dst, mate) for mate in mates]
        for copy in copies:
            copy.start()
        return copies

    plane_copies = to_all(plane.at[gy, me], plane.at[gy, me], plane_mates)
    tile_copy = remote(other, halo.at[(2,) + inner], (gy, gx, 1 - me))
    tile_copy.start()
    rims = []
    for dy, dx in compass:
        src = (spots(dy, tile_h, False), spots(dx, tile_w, False))
        dst = (spots(dy, tile_h, True), spots(dx, tile_w, True))
        both = [
            remote(
                same.at[(slice(None),) + src], halo.at[(pl.ds(0, 2),) + dst],
                (gy + dy, gx + dx, me),
            ),
            remote(other.at[src], halo.at[(2,) + dst], (gy + dy, gx + dx, 1 - me)),
        ]
        rims.append((dy, dx, both))

        @pl.when(exists(dy, dx))
        def _():
            for copy in both:
                copy.start()

    for copy in plane_copies:
        copy.wait()
    for which in range(2):
        total = plane[0, which]
        for k in range(1, ny):
            total = total + plane[k, which]
        line[gx, which] = total
    line_copies = to_all(line.at[gx], line.at[gx], line_mates)
    rest_copy = remote(same.at[1], rest, (gy, gx, 1 - me))
    rest_copy.start()
    for copy in line_copies:
        copy.wait()

    def moments(which):
        total = line[0, which]
        for k in range(1, nx):
            total = total + line[k, which]
        total = total / count
        valid = lax.broadcasted_iota(jnp.int32, total.shape, 1) < GROUPS
        return [
            jnp.where(valid, total if k == 0 else pltpu.roll(total, lanes - GROUPS * k, 1), 0.0)
            for k in range(4)
        ]

    mean_x, mean_xx, mean_u, cross = moments(me)
    _, _, mean_v, cross_v = moments(1 - me)
    inv = 1.0 / jnp.sqrt(mean_xx - mean_x * mean_x + 1e-05)
    cube = inv * inv * inv
    table = jnp.concatenate(
        [mean_x, inv, mean_u, (cross - mean_x * mean_u) * cube, mean_v,
         (cross_v - mean_x * mean_v) * cube], axis=0,
    )
    chan = lax.broadcasted_iota(jnp.int32, (lanes, share), 1) + me * share
    group = lax.broadcasted_iota(jnp.int32, (lanes, share), 0) * width
    spread = ((chan >= group) & (chan < group + width)).astype(F32)
    table = exact_dot(table, spread)
    mean_x, inv, mean_u, mean_cu, mean_v, mean_cv = [
        table[k * rows : (k + 1) * rows] for k in range(6)
    ]
    for copy in inputs[2:6]:
        copy.wait()
    embed = jnp.concatenate(
        [time_ref[pl.ds(steps_ref[b], 1), :] for b in range(batch)] * probes, axis=0
    )
    offset = half(embed + shift_ref[...].reshape(1, chans), me)
    gain = half(jnp.broadcast_to(gain_ref[...].reshape(1, chans), (rows, chans)), me)

    tile_copy.wait()
    for dy, dx, both in rims:
        @pl.when(exists(dy, dx))
        def _():
            for copy in both:
                copy.wait_send()

        @pl.when(exists(-dy, -dx))
        def _():
            for copy in both:
                copy.wait_recv()

    for y in range(tile_h + 2):
        centered = halo[0, y].astype(F32) - mean_x
        normal = centered * inv
        pre = normal * gain + offset
        sig = 1.0 / (1.0 + jnp.exp(-pre))
        slope = sig * (1.0 + pre * (1.0 - sig)) * gain
        acts[y, :, 0:rows] = pre * sig
        acts[y, :, rows : 2 * rows] = slope * (
            (halo[1, y].astype(F32) - mean_u) * inv - centered * mean_cu
        )
        acts[y, :, 2 * rows :] = slope * (
            (halo[2, y].astype(F32) - mean_v) * inv - centered * mean_cv
        )
    for edge, at in (
        (gy == 0, (0,)), (gy == ny - 1, (tile_h + 1,)),
        (gx == 0, (slice(None), 0)), (gx == nx - 1, (slice(None), tile_w + 1)),
    ):
        @pl.when(edge)
        def _():
            acts[at] = jnp.zeros(acts.at[at].shape, F32)

    def conv(first, size):
        for tap in range(9):
            dy, dx = tap // 3, tap % 3
            window = acts[dy : dy + tile_h, dx : dx + tile_w, first : first + size]
            cols[: cells * size, tap * share : (tap + 1) * share] = window.reshape(
                cells * size, share
            ).astype(BF16)
        total = jnp.dot(cols[: cells * size], w_ref[...], preferred_element_type=F32)
        return total.reshape(cells, size, chans)

    inputs[6].wait()
    vel[...] = conv(0, rows)[:, :batch]
    vel_copy = remote(vel, vel_in, (gy, gx, 1 - me))
    vel_copy.start()
    tangent = conv(rows, 2 * rows).reshape(cells * 2 * rows, chans)
    rest_copy.wait()

    def pairs(at):
        return at.astype(F32).reshape(cells, rows, share)

    near = half(tangent, me).reshape(cells, 2 * rows, share)
    far = half(tangent, 1 - me).reshape(cells, 2 * rows, share)
    product = jnp.sum(
        pairs(same[1]) * near[:, :rows] + pairs(halo[(2,) + inner]) * near[:, rows:]
        + pairs(other[...]) * far[:, :rows] + pairs(rest[...]) * far[:, rows:],
        axis=0,
    )
    product = jnp.sum(product, axis=1, keepdims=True)
    lane = lax.broadcasted_iota(jnp.int32, (rows, lanes), 1)
    row = lax.broadcasted_iota(jnp.int32, (rows, lanes), 0)
    here = jnp.where(lane == lax.rem(row, batch), product, 0.0)
    mine = (gy * nx + gx) * 2 + me
    parts[mine] = jnp.sum(here, axis=0, keepdims=True)
    everyone = [
        (lax.rem(gy + a, ny), lax.rem(gx + b, nx), lax.rem(me + q, 2))
        for a in range(ny) for b in range(nx) for q in range(2) if a or b or q
    ]
    copies = to_all(parts.at[mine], parts.at[mine], everyone)
    vel_copy.wait()
    vel[...] = 0.25 * (vel[...] + vel_in[...] + bias_ref[...].reshape(1, chans))
    for b in range(batch):
        for y in range(tile_h):
            moved = vel[y * tile_w : (y + 1) * tile_w, b, :]
            out[b, y] = (state_f[b, y] + moved).astype(BF16)
    for copy in copies:
        copy.wait()
    l_out[...] = jnp.sum(parts[...], axis=0) * (-0.25 / (2 * probes))


def settle(state_ref, total_ref, state_out, total_out):
    state_out[...] = state_ref[...]
    total_out[...] = total_ref[0, : total_out.shape[0]]


def one_kernel(state, probe_signs, timesteps, time_table, gn_gain, gn_shift, conv_weight, conv_bias):
    batch, tile_h, tile_w, chans = state.shape
    probes = probe_signs.shape[0]
    share = conv_weight.shape[1]
    ny, nx = lax.axis_size("gy"), lax.axis_size("gx")
    rows = probes * batch
    cells = tile_h * tile_w
    copies = (nx - 1) + (2 * ny - 1) + 3 + 16 + (2 * nx * ny - 1)
    vmem = pl.BlockSpec(memory_space=pltpu.VMEM)
    hbm = pl.BlockSpec(memory_space=pl.ANY)
    next_state, total = pl.pallas_call(
        functools.partial(kernel, ny, nx),
        out_shape=(
            jax.ShapeDtypeStruct(state.shape, BF16),
            jax.ShapeDtypeStruct((1, 128), F32),
        ),
        in_specs=[pl.BlockSpec(memory_space=pltpu.SMEM)] + [hbm] * 7,
        out_specs=(vmem, vmem),
        scratch_shapes=[
            pltpu.VMEM(state.shape, BF16),
            pltpu.VMEM(probe_signs.shape, jnp.int32),
            pltpu.VMEM(time_table.shape, F32),
            pltpu.VMEM(gn_gain.shape, F32),
            pltpu.VMEM(gn_shift.shape, F32),
            pltpu.VMEM(conv_bias.shape, F32),
            pltpu.VMEM((9 * share, chans), BF16),
            pltpu.VMEM(state.shape, F32),
            pltpu.VMEM((3, tile_h + 2, tile_w + 2, rows, share), BF16),
            pltpu.VMEM((2, tile_h, tile_w, rows, share), BF16),
            pltpu.VMEM((tile_h, tile_w, rows, share), BF16),
            pltpu.VMEM((tile_h, tile_w, rows, share), BF16),
            pltpu.VMEM((tile_h + 2, tile_w + 2, 3 * rows, share), F32),
            pltpu.VMEM((cells * 2 * rows, 9 * share), BF16),
            pltpu.VMEM((nx, 2, rows, 128), F32),
            pltpu.VMEM((ny, 2, rows, 128), F32),
            pltpu.VMEM((cells, batch, chans), F32),
            pltpu.VMEM((cells, batch, chans), F32),
            pltpu.VMEM((2 * nx * ny, 1, 128), F32),
            pltpu.SemaphoreType.DMA((7,)),
            pltpu.SemaphoreType.DMA((copies,)),
            pltpu.SemaphoreType.DMA((copies,)),
        ],
        compiler_params=pltpu.CompilerParams(collective_id=0, has_side_effects=True),
    )(
        timesteps, state, probe_signs, time_table, gn_gain,
        gn_shift, conv_bias,
        conv_weight.reshape(9 * share, chans),
    )
    return pl.pallas_call(
        settle,
        out_shape=(
            jax.ShapeDtypeStruct(state.shape, BF16), jax.ShapeDtypeStruct((batch,), F32)
        ),
        in_specs=[vmem, vmem],
        out_specs=(vmem, vmem),
    )(next_state, total)


def solution(mesh):
    def body(*args):
        wide = mesh.shape["probe"] == 2 and args[6].shape[1] >= 128
        rows = args[1].shape[0] * args[0].shape[0]
        return (one_kernel if wide and rows == 8 else gathered_weights)(*args)

    in_specs = (
        P(None, "gy", "gx", None),
        P("probe", None, "gy", "gx", None),
        P(),
        P(),
        P(),
        P(),
        P(None, "probe", None),
        P(),
    )
    out_specs = (P(None, "gy", "gx", None), P())
    return jax.shard_map(body, mesh=mesh, in_specs=in_specs, out_specs=out_specs, check_vma=False)
```
